32 devices in a mesh: fields: 2 (over x), prow: 8 (over z, y), pcol: 2 (over core).
Axes of the slice: x: 2, y: 2, z: 4, core: 2. Of those that a mesh axis runs over, the one named last changes fastest.
Arguments:
- inverse_tiles: bfloat16 [32, 16, 256, 256], P(('fields', 'prow'), 'pcol'), parts along dimension 0, may hold values from -6 to 6
- panel_blocks: bfloat16 [4, 8, 256, 512], P('fields', 'prow', None, 'pcol'), parts along dimension 0, may hold values from -0.125 to 0.125
- diag_inverse: float32 [4, 512], P('fields', 'pcol'), parts along dimension 0, may hold values from 0.5 to 2
- structure: int32 [4, 8], P('fields'), parts along dimension 0, may hold values from 0 to 15, as said below
- block_slot: int32 [32], P('fields'), parts along dimension 0, may hold values from 0 to 15, each once
Outputs:
- sigma_new: bfloat16 [4, 16, 256, 512], P('fields', 'prow', None, 'pcol'), parts along dimension 0
- variances: float32 [4, 512], P('fields', 'pcol'), parts along dimension 0
The draws below stay inside these ranges and needn't reach their ends.
There are 2 independent parts, one for each index of `fields`. The reference program is written for one: setup_inputs(seed, part) draws one part's arguments, and reference() takes and returns one part's arrays. A program takes and returns all parts, laid end to end along the dimension named above; each array names one. Nothing has to cross between parts.
Inputs may be any that keep to these rules, and one draw needn't show every extreme that they name: `structure`: each row lists 8 distinct row blocks in increasing order, and the last is always 16 - 1. `block_slot`: each slot is used by exactly one row block.
All inputs are finite; a program needn't handle non-finite values.
Results may differ from the reference program's by a relative error of at most 0.0006.
Values may be sent and summed in bfloat16 or wider, within the bound.
No kernel may reach another device: no remote copies, remote signals or barrier semaphores. Data moves between devices by JAX's collectives and lax.ppermute only.
A program may use at most 128 MiB of HBM per device.

```python
import math
import jax
import jax.numpy as jnp
from jax import lax

W = 512
B = 256
NSUP = 2
NB = 16
R = 8


def draw_structure(key, part):

    def single_list(subkey):
        order = jax.random.permutation(subkey, NB - 1).astype(jnp.int32)
        chosen = jnp.concatenate([order[:R - 1], jnp.full((1,), NB - 1, jnp.int32)])
        return jnp.sort(chosen)
    keys = jax.random.split(jax.random.fold_in(key, 7), NSUP)
    return jax.vmap(single_list)(keys)


def shard_levels(stream_key, extent, pieces, least, top_value):
    def one(axis_at, shards_of):
        draws = jax.random.uniform(jax.random.fold_in(jax.random.fold_in(stream_key, 6), axis_at), (shards_of,), jnp.float32, least / len(pieces), top_value / len(pieces))
        return jnp.repeat(jnp.exp(draws), extent[axis_at] // shards_of).reshape((-1,) + (1,) * (len(extent) - axis_at - 1))

    gain = one(*pieces[0])
    for cut in pieces[1:]:
        gain = gain * one(*cut)
    return gain


def centred(stream_key, extent, width, limit, cuts=(), kind=jnp.bfloat16):
    loudness = shard_levels(stream_key, extent, cuts, -0.22, 0.18) if cuts else 1.0
    values = jax.random.normal(stream_key, extent, jnp.float32) * width * loudness
    return jnp.minimum(jnp.maximum(values, -limit), limit).astype(kind)


def setup_inputs(seed: int = 0, part: int = 0) -> dict:
    arg_keys = jax.random.split(jax.random.key(seed), 6)
    part_splits = jax.random.split(jax.random.fold_in(arg_keys[5], part), 6)
    return {
        "inverse_tiles": centred(part_splits[0], (NB, NB, B, B), 1.0, 6.0, ((0, 8), (1, 2))),
        "panel_blocks": centred(part_splits[1], (NSUP, R, B, W), (R * B) ** -0.5, 0.125, ((1, 8), (3, 2))),
        "diag_inverse": jnp.clip(jnp.exp(math.log(2.0) - 1.3862944 * jax.random.uniform(part_splits[2], (NSUP, W), jnp.float32) ** shard_levels(part_splits[2], (NSUP, W), ((1, 2),), -0.2, 0.2)), 0.5, 2.0),
        "structure": draw_structure(jax.random.fold_in(jax.random.fold_in(arg_keys[5], part), 71), part),
        "block_slot": jax.random.permutation(part_splits[4], NB).astype(jnp.int32),
    }


def reference(inverse_tiles, panel_blocks, diag_inverse, structure, block_slot):
    sigma_list = []
    variance_list = []
    for sup_index in range(NSUP):
        slot_of = block_slot[structure[sup_index]].astype(jnp.int32)
        gathered = inverse_tiles[slot_of][:, slot_of].astype(jnp.float32)
        panel_full = panel_blocks[sup_index].astype(jnp.float32)
        sigma_rows = -jnp.einsum("abxy,byw->axw", gathered, panel_full, precision=lax.Precision.HIGHEST)
        stored = jnp.zeros((NB, B, W), jnp.bfloat16).at[slot_of].set(sigma_rows.astype(jnp.bfloat16))
        variance = diag_inverse[sup_index] - jnp.einsum("axw,axw->w", panel_full, sigma_rows, precision=lax.Precision.HIGHEST)
        sigma_list.append(stored)
        variance_list.append(variance)
    return jnp.stack(sigma_list), jnp.stack(variance_list)
```

```python
import functools
import jax
import jax.numpy as jnp
from jax import lax
from jax.experimental import pallas as pl
from jax.experimental.pallas import tpu as pltpu
from jax.sharding import PartitionSpec as P

AXES = ("prow", "pcol")


def ring_order(size):
    return list(range(0, size, 2)) + [i for i in range(size - 1, 0, -1) if i % 2]


def ring_pairs(size):
    order = ring_order(size)
    pairs = []
    for place, row in enumerate(order):
        pairs.append((row * 2, order[(place + 1) % size] * 2))
        pairs.append((row * 2 + 1, order[(place - 1) % size] * 2 + 1))
    return pairs


def accumulate_kernel(count, tail, idx, structure, block_slot, own_inv, other_inv, *refs):
    panels = refs[:count]
    acc, own_panel, tail_tiles, tiles, pcat, tile_sem, panel_sem, tail_sem = refs[count:]
    supers, size = pcat.shape[0], pcat.shape[2]
    rows, cols = own_inv.shape[0], own_inv.shape[1]
    per = panels[0].shape[1]
    me_col = idx[1]

    def copy_tiles(slot, dst, sem):
        mine = slot // cols == me_col
        at = lax.rem(slot, cols)
        for r in range(rows):
            @pl.when(mine)
            def _():
                pltpu.make_async_copy(own_inv.at[r, at], dst(r), sem).start()

            @pl.when(jnp.logical_not(mine))
            def _():
                pltpu.make_async_copy(other_inv.at[r, at], dst(r), sem).start()

    for j in range(count):
        for s in range(supers):
            for k in range(per):
                pltpu.make_async_copy(panels[j].at[s, k], pcat.at[s, j * per + k], panel_sem.at[j]).start()
                slot = block_slot[structure[s, idx[2 + j] * per + k]]
                copy_tiles(slot, lambda r: tiles.at[s, j * per + k, pl.ds(r * size, size)], tile_sem.at[j])
    for j in range(tail):
        for s in range(supers):
            for k in range(per):
                slot = block_slot[structure[s, idx[2 + count + j] * per + k]]
                copy_tiles(slot, lambda r: tail_tiles.at[s, j * per + k, pl.ds(r * size, size)], tail_sem)
    for j in range(count):
        here = pl.ds(j * per, per)
        pltpu.make_async_copy(tiles.at[:, here], tiles.at[:, here], tile_sem.at[j]).wait()
        pltpu.make_async_copy(pcat.at[:, here], pcat.at[:, here], panel_sem.at[j]).wait()
        for s in range(supers):
            for k in range(per):
                part = jnp.dot(tiles[s, j * per + k], pcat[s, j * per + k], preferred_element_type=jnp.float32)
                if j == 0 and k == 0:
                    acc[s] = part
                else:
                    acc[s] += part
    for s in range(supers):
        for r in range(rows):
            row = idx[0] * rows + r
            where = jnp.int32(0)
            found = jnp.int32(0)
            for j in range(count):
                for k in range(per):
                    hit = (block_slot[structure[s, idx[2 + j] * per + k]] == row).astype(jnp.int32)
                    where = where + hit * (j * per + k)
                    found = found + hit
            own_panel[s, pl.ds(r * size, size)] = jnp.where(
                found > 0, pcat[s, where], jnp.zeros((), own_panel.dtype)
            )
    pltpu.make_async_copy(tail_tiles, tail_tiles, tail_sem).wait()


def finish_kernel(count, tail, idx, structure, block_slot, acc, own_panel, tail_tiles, diag, *refs):
    panels = refs[:tail]
    sigma, value = refs[tail:]
    supers, size = acc.shape[0], acc.shape[2]
    rows = acc.shape[1] // size
    per = panels[0].shape[1]
    first = (idx[0] == 0).astype(jnp.float32)
    for s in range(supers):
        total = acc[s]
        for j in range(tail):
            for k in range(per):
                total = total + jnp.dot(
                    tail_tiles[s, j * per + k], panels[j][s, k], preferred_element_type=jnp.float32
                )
        result = diag[pl.ds(s, 1)] * first
        for r in range(rows):
            row = idx[0] * rows + r
            used = jnp.bool_(False)
            for b in range(structure.shape[1]):
                used = jnp.logical_or(used, block_slot[structure[s, b]] == row)
            one = jnp.where(used, -total[r * size:(r + 1) * size], 0.0)
            panel = own_panel[s, pl.ds(r * size, size)].astype(jnp.float32)
            for j in range(tail):
                for k in range(per):
                    hit = block_slot[structure[s, idx[2 + count + j] * per + k]] == row
                    panel = jnp.where(hit, panels[j][s, k].astype(jnp.float32), panel)
            result = result - jnp.sum(panel * one, axis=0, keepdims=True)
            sigma[s, r] = one.astype(sigma.dtype)
        value[pl.ds(s, 1)] = result


def per_device(grid_rows, inverse_tiles, panel_blocks, diag_inverse, structure, block_slot):
    rows, cols, size = inverse_tiles.shape[0], inverse_tiles.shape[1], inverse_tiles.shape[2]
    supers, per = panel_blocks.shape[0], panel_blocks.shape[1]
    pairs = ring_pairs(grid_rows)
    swap = [(i, i ^ 1) for i in range(2 * grid_rows)]
    hop = lambda x: lax.ppermute(x, AXES, pairs)
    cross = lambda x: lax.ppermute(x, AXES, swap)

    mine = hop(panel_blocks)
    theirs_now = cross(panel_blocks)
    other_inverse = cross(inverse_tiles)
    along, across = [mine], []
    for step in range(1, grid_rows // 2 + 1):
        if step <= (grid_rows - 1) // 2:
            theirs_now = hop(theirs_now)
        if step < grid_rows // 2:
            mine = hop(mine)
            along.append(mine)
        if step <= (grid_rows - 1) // 2:
            across.append(cross(theirs_now))

    prow, pcol = lax.axis_index("prow"), lax.axis_index("pcol")
    order = jnp.array(ring_order(grid_rows), jnp.int32)
    half = (grid_rows + 1) // 2
    place = jnp.where(prow % 2 == 0, prow // 2, grid_rows - 1 - prow // 2)
    sign = jnp.where(pcol == 0, -1, 1)

    def row_at(offset):
        at = lax.rem(place + offset + grid_rows, grid_rows)
        return jnp.where(at < half, 2 * at, 2 * (grid_rows - 1 - at) + 1)

    shards = [(panel_blocks, prow)]
    for k in range(1, grid_rows // 2 + 1):
        shards.append((along[k - 1], row_at(sign * k)))
        if k <= (grid_rows - 1) // 2:
            shards.append((across[k - 1], row_at(-sign * k)))
    tail = 2
    count = len(shards) - tail
    idx = jnp.stack([prow, pcol] + [i for _, i in shards]).astype(jnp.int32)

    smem = pl.BlockSpec(memory_space=pltpu.SMEM)
    vmem = pl.BlockSpec(memory_space=pltpu.VMEM)
    hbm = pl.BlockSpec(memory_space=pl.ANY)
    tile = size * size
    acc, own_panel, tail_tiles = pl.pallas_call(
        functools.partial(accumulate_kernel, count, tail),
        out_shape=(
            jax.ShapeDtypeStruct((supers, rows * size, size), jnp.float32),
            jax.ShapeDtypeStruct((supers, rows * size, size), jnp.bfloat16),
            jax.ShapeDtypeStruct((supers, tail * per, rows * size, size), jnp.bfloat16),
        ),
        in_specs=[smem] * 3 + [hbm] * (2 + count),
        out_specs=(vmem, vmem, vmem),
        scratch_shapes=[
            pltpu.VMEM((supers, count * per, rows * size, size), jnp.bfloat16),
            pltpu.VMEM((supers, count * per, size, size), jnp.bfloat16),
            pltpu.SemaphoreType.DMA((count,)),
            pltpu.SemaphoreType.DMA((count,)),
            pltpu.SemaphoreType.DMA,
        ],
        cost_estimate=pl.CostEstimate(
            flops=2 * supers * count * per * rows * tile * size,
            bytes_accessed=2 * supers * (count + tail) * per * (rows + 1) * tile,
            transcendentals=0,
        ),
        name="accumulate",
    )(idx, structure, block_slot, inverse_tiles, other_inverse, *[x for x, _ in shards[:count]])

    sigma, value = pl.pallas_call(
        functools.partial(finish_kernel, count, tail),
        out_shape=(
            jax.ShapeDtypeStruct((supers, rows, size, size), jnp.bfloat16),
            jax.ShapeDtypeStruct(diag_inverse.shape, jnp.float32),
        ),
        in_specs=[smem] * 3 + [vmem] * (4 + tail),
        out_specs=(vmem, vmem),
        cost_estimate=pl.CostEstimate(
            flops=2 * supers * tail * per * rows * tile * size,
            bytes_accessed=supers * rows * tile * 8,
            transcendentals=0,
        ),
        name="finish",
    )(idx, structure, block_slot, acc, own_panel, tail_tiles, diag_inverse, *[x for x, _ in shards[count:]])

    stride = 1
    while stride < grid_rows:
        value = value + lax.ppermute(value, "prow", [(i, i ^ stride) for i in range(grid_rows)])
        stride *= 2
    return sigma, value


def solution(mesh):
    in_specs = (
        P(("fields", "prow"), "pcol", None, None),
        P("fields", "prow", None, "pcol"),
        P("fields", "pcol"),
        P("fields", None),
        P("fields"),
    )
    out_specs = (P("fields", "prow", None, "pcol"), P("fields", "pcol"))
    return jax.shard_map(
        functools.partial(per_device, mesh.shape["prow"]),
        mesh=mesh,
        in_specs=in_specs,
        out_specs=out_specs,
        check_vma=False,
    )
```

```python
import functools
import jax
import jax.numpy as jnp
from jax import lax
from jax.experimental import pallas as pl
from jax.experimental.pallas import tpu as pltpu
from jax.sharding import PartitionSpec as P

AXES = ("prow", "pcol")


def ring_order(size):
    return list(range(0, size, 2)) + [i for i in range(size - 1, 0, -1) if i % 2]


def ring_pairs(size):
    order = ring_order(size)
    pairs = []
    for place, row in enumerate(order):
        pairs.append((row * 2, order[(place + 1) % size] * 2))
        pairs.append((row * 2 + 1, order[(place - 1) % size] * 2 + 1))
    return pairs


class Place:
    def __init__(self, size):
        self.size = size
        self.prow = lax.axis_index("prow")
        self.pcol = lax.axis_index("pcol")
        odd = self.prow & 1
        half = self.prow >> 1
        self.at = half + odd * (size - 1 - 2 * half)

    def row(self, steps):
        if steps == 0:
            return self.prow
        at = lax.rem(self.at + self.size - steps * (1 - 2 * self.pcol), self.size)
        return jnp.where(2 * at < self.size, 2 * at, 2 * (self.size - 1 - at) + 1)


def load_kernel(source, target, sem):
    copy = pltpu.make_async_copy(source, target, sem)
    copy.start()
    copy.wait()


def add_products(place, steps, structure, block_slot, own, other, panels, acc, fresh):
    rows, cols, size = own.shape[0], own.shape[1], own.shape[2]
    for j, panel in enumerate(panels):
        shard_row = place.row(steps[j])
        per = panel.shape[1]
        for s in range(panel.shape[0]):
            for k in range(per):
                slot = block_slot[structure[s, shard_row * per + k]]
                mine = slot // cols == place.pcol
                at = lax.rem(slot, cols)
                for r in range(rows):
                    tile = jnp.where(mine, own[r, at], other[r, at])
                    part = jnp.dot(tile, panel[s, k], preferred_element_type=jnp.float32)
                    here = pl.ds(r * size, size)
                    if fresh and j == 0 and k == 0:
                        acc[s, here] = part
                    else:
                        acc[s, here] += part


def panel_hits(place, steps, structure, block_slot, panels, rows, s, r):
    per = panels[0].shape[1]
    for j, panel in enumerate(panels):
        for k in range(per):
            yield block_slot[structure[s, place.row(steps[j]) * per + k]] == place.prow * rows + r, panel, k


def accumulate_kernel(grid_rows, steps, structure, block_slot, own, other, *refs):
    panels, (acc, own_panel) = refs[:len(steps)], refs[len(steps):]
    place = Place(grid_rows)
    rows, size = own.shape[0], own.shape[2]
    own_panel[...] = jnp.zeros_like(own_panel)
    for s in range(acc.shape[0]):
        for r in range(rows):
            for hit, panel, k in panel_hits(place, steps, structure, block_slot, panels, rows, s, r):
                @pl.when(hit)
                def _():
                    own_panel[s, pl.ds(r * size, size)] = panel[s, k]
    add_products(place, steps, structure, block_slot, own, other, panels, acc, True)


def finish_kernel(grid_rows, steps, structure, block_slot, own, other, acc, own_panel, diag, *refs):
    panels, (sigma, value, total, panel_rows) = refs[:len(steps)], refs[len(steps):]
    place = Place(grid_rows)
    rows, size = own.shape[0], own.shape[2]
    supers = acc.shape[0]
    total[...] = acc[...]
    panel_rows[...] = own_panel[...]
    add_products(place, steps, structure, block_slot, own, other, panels, total, False)
    first = (place.prow == 0).astype(jnp.float32)
    for s in range(supers):
        result = diag[pl.ds(s, 1)] * first
        for r in range(rows):
            here = pl.ds(r * size, size)
            for hit, panel, k in panel_hits(place, steps, structure, block_slot, panels, rows, s, r):
                @pl.when(hit)
                def _():
                    panel_rows[s, here] = panel[s, k]
            used = jnp.bool_(False)
            for b in range(structure.shape[1]):
                used = jnp.logical_or(used, block_slot[structure[s, b]] == place.prow * rows + r)
            one = jnp.where(used, -total[s, here], 0.0)
            result = result - jnp.sum(panel_rows[s, here].astype(jnp.float32) * one, axis=0, keepdims=True)
            sigma[s, r] = one.astype(sigma.dtype)
        value[pl.ds(s, 1)] = result


def per_device(grid_rows, inverse_tiles, panel_blocks, diag_inverse, structure, block_slot):
    rows, size = inverse_tiles.shape[0], inverse_tiles.shape[2]
    supers, per = panel_blocks.shape[0], panel_blocks.shape[1]
    pairs = ring_pairs(grid_rows)
    swap = [(i, i ^ 1) for i in range(2 * grid_rows)]
    ways, backs = grid_rows // 2, (grid_rows - 1) // 2

    def hop(x):
        return lax.ppermute(x, AXES, pairs)

    def cross(x):
        return lax.ppermute(x, AXES, swap)

    smem = pl.BlockSpec(memory_space=pltpu.SMEM)
    vmem = pl.BlockSpec(memory_space=pltpu.VMEM)
    hbm = pl.BlockSpec(memory_space=pltpu.HBM)

    mine = hop(panel_blocks)
    theirs = cross(panel_blocks)
    own = pl.pallas_call(
        load_kernel,
        out_shape=jax.ShapeDtypeStruct(inverse_tiles.shape, inverse_tiles.dtype),
        in_specs=[hbm],
        out_specs=vmem,
        scratch_shapes=[pltpu.SemaphoreType.DMA],
        compiler_params=pltpu.CompilerParams(vmem_limit_bytes=4 << 20),
        name="load",
    )(inverse_tiles)
    other = cross(inverse_tiles)
    shards = [(0, panel_blocks), (1, mine)]
    for step in range(1, ways + 1):
        if step <= backs:
            theirs = hop(theirs)
        if step < ways:
            mine = hop(mine)
        if step <= backs:
            shards.append((-step, cross(theirs)))
        if step < ways:
            shards.append((step + 1, mine))
    tail = min(2, len(shards) - 1)
    count = len(shards) - tail
    early, late = shards[:count], shards[count:]

    tile = size * size
    small = pltpu.CompilerParams(vmem_limit_bytes=8 << 20)
    acc, own_panel = pl.pallas_call(
        functools.partial(accumulate_kernel, grid_rows, [k for k, _ in early]),
        out_shape=(
            jax.ShapeDtypeStruct((supers, rows * size, size), jnp.float32),
            jax.ShapeDtypeStruct((supers, rows * size, size), jnp.bfloat16),
        ),
        in_specs=[smem] * 2 + [vmem] * (2 + count),
        out_specs=(vmem, vmem),
        compiler_params=small,
        cost_estimate=pl.CostEstimate(
            flops=2 * supers * count * per * rows * tile * size,
            bytes_accessed=2 * supers * count * per * (rows + 1) * tile,
            transcendentals=0,
        ),
        name="accumulate",
    )(structure, block_slot, own, other, *[x for _, x in early])

    sigma, value = pl.pallas_call(
        functools.partial(finish_kernel, grid_rows, [k for k, _ in late]),
        out_shape=(
            jax.ShapeDtypeStruct((supers, rows, size, size), jnp.bfloat16),
            jax.ShapeDtypeStruct(diag_inverse.shape, jnp.float32),
        ),
        in_specs=[smem] * 2 + [vmem] * (5 + tail),
        out_specs=(vmem, vmem),
        scratch_shapes=[
            pltpu.VMEM((supers, rows * size, size), jnp.float32),
            pltpu.VMEM((supers, rows * size, size), jnp.bfloat16),
        ],
        compiler_params=small,
        cost_estimate=pl.CostEstimate(
            flops=2 * supers * tail * per * rows * tile * size,
            bytes_accessed=supers * rows * tile * 8,
            transcendentals=0,
        ),
        name="finish",
    )(structure, block_slot, own, other, acc, own_panel, diag_inverse, *[x for _, x in late])

    stride = 1
    while stride < grid_rows:
        value = value + lax.ppermute(value, "prow", [(i, i ^ stride) for i in range(grid_rows)])
        stride *= 2
    return sigma, value


def solution(mesh):
    in_specs = (
        P(("fields", "prow"), "pcol", None, None),
        P("fields", "prow", None, "pcol"),
        P("fields", "pcol"),
        P("fields", None),
        P("fields"),
    )
    out_specs = (P("fields", "prow", None, "pcol"), P("fields", "pcol"))
    grid_rows = mesh.shape["prow"]

    def body(*args):
        return per_device(grid_rows, *args)

    return jax.shard_map(body, mesh=mesh, in_specs=in_specs, out_specs=out_specs, check_vma=False)
```

```python
import functools
import jax
import jax.numpy as jnp
from jax import lax
from jax.experimental import pallas as pl
from jax.experimental.pallas import tpu as pltpu
from jax.sharding import PartitionSpec as P

AXES = ("prow", "pcol")


def ring_order(size):
    return list(range(0, size, 2)) + [i for i in range(size - 1, 0, -1) if i % 2]


def ring_pairs(size):
    order = ring_order(size)
    pairs = []
    for place, row in enumerate(order):
        pairs.append((row * 2, order[(place + 1) % size] * 2))
        pairs.append((row * 2 + 1, order[(place - 1) % size] * 2 + 1))
    return pairs


class Place:
    def __init__(self, size):
        self.size = size
        self.prow = lax.axis_index("prow")
        self.pcol = lax.axis_index("pcol")
        odd = self.prow & 1
        half = self.prow >> 1
        self.at = half + odd * (size - 1 - 2 * half)

    def row(self, steps):
        if steps == 0:
            return self.prow
        at = lax.rem(self.at + self.size - steps * (1 - 2 * self.pcol), self.size)
        return jnp.where(2 * at < self.size, 2 * at, 2 * (self.size - 1 - at) + 1)


def load_kernel(source, target, sem):
    copy = pltpu.make_async_copy(source, target, sem)
    copy.start()
    copy.wait()


def prepare_kernel(grid_rows, s, late, structure, block_slot, own, other, late_tiles, marks):
    place = Place(grid_rows)
    rows, cols, size = own.shape[0], own.shape[1], own.shape[2]
    count = late_tiles.shape[0]
    per = count // len(late)
    slots = [block_slot[structure[s, place.row(k) * per + i]] for k in late for i in range(per)]
    every = [block_slot[structure[s, b]] for b in range(structure.shape[1])]
    for r in range(rows):
        row = place.prow * rows + r
        used = functools.reduce(jnp.logical_or, [slot == row for slot in every])
        marks[pl.ds(r, 1)] = jnp.full((1, size), -used.astype(jnp.float32))
        for i, slot in enumerate(slots):
            hit = (slot == row).astype(jnp.float32)
            marks[pl.ds(rows + i * rows + r, 1)] = jnp.full((1, size), hit)
    for i, slot in enumerate(slots):
        at = lax.rem(slot, cols)
        for r in range(rows):
            late_tiles[i, pl.ds(r * size, size)] = jnp.where(slot // cols == place.pcol, own[r, at], other[r, at])


def add_kernel(grid_rows, steps, fresh, structure, block_slot, own, other, *refs):
    panels, (acc, own_panel) = refs[:len(steps)], refs[-2:]
    place = Place(grid_rows)
    rows, cols, size = own.shape[0], own.shape[1], own.shape[2]
    supers, per = panels[0].shape[0], panels[0].shape[1]
    if fresh:
        own_panel[...] = jnp.zeros_like(own_panel)
    shard_rows = [place.row(k) * per for k in steps]
    blocks = [(panel, k) for panel in panels for k in range(per)]
    slots = [[block_slot[structure[s, at + k]] for at in shard_rows for k in range(per)] for s in range(supers)]
    for s in range(supers):
        for r in range(rows):
            for slot, (panel, k) in zip(slots[s], blocks):

                @pl.when(slot == place.prow * rows + r)
                def _():
                    own_panel[s, pl.ds(r * size, size)] = panel[s, k]

    for s in range(supers):
        for r in range(rows):
            here = pl.ds(r * size, size)
            total = None if fresh else acc[s, here]
            for slot, (panel, k) in zip(slots[s], blocks):
                at = lax.rem(slot, cols)
                tile = jnp.where(slot // cols == place.pcol, own[r, at], other[r, at])
                part = jnp.dot(tile, panel[s, k], preferred_element_type=jnp.float32)
                total = part if total is None else total + part
            acc[s, here] = total


def finish_kernel(supers, count, diag, first, acc, own_panel, *refs):
    tiles, marks, refs = refs[:supers], refs[supers:2 * supers], refs[2 * supers:]
    panels, (sigma, value) = refs[:-2], refs[-2:]
    rows, size = sigma.shape[1], sigma.shape[2]
    blocks = [(panel, k) for panel in panels for k in range(count // len(panels))]
    for s in range(supers):
        result = diag[pl.ds(s, 1)] * first[...]
        for r in range(rows):
            here = pl.ds(r * size, size)
            total = acc[s, here]
            for i, (panel, k) in enumerate(blocks):
                total = total + jnp.dot(tiles[s][i, here], panel[s, k], preferred_element_type=jnp.float32)
            total = total * marks[s][pl.ds(r, 1)]
            sigma[s, r] = total.astype(sigma.dtype)
            weight = own_panel[s, here].astype(jnp.float32)
            for i, (panel, k) in enumerate(blocks):
                weight = weight + marks[s][pl.ds(rows + i * rows + r, 1)] * panel[s, k].astype(jnp.float32)
            result = result - jnp.sum(weight * total, axis=0, keepdims=True)
        value[pl.ds(s, 1)] = result


def per_device(grid_rows, inverse_tiles, panel_blocks, diag_inverse, structure, block_slot):
    rows, size = inverse_tiles.shape[0], inverse_tiles.shape[2]
    supers, per = panel_blocks.shape[0], panel_blocks.shape[1]
    pairs = ring_pairs(grid_rows)
    swap = [(i, i ^ 1) for i in range(2 * grid_rows)]
    ways, backs = grid_rows // 2, (grid_rows - 1) // 2

    def hop(x):
        return lax.ppermute(x, AXES, pairs)

    def cross(x):
        return lax.ppermute(x, AXES, swap)

    smem = pl.BlockSpec(memory_space=pltpu.SMEM)
    vmem = pl.BlockSpec(memory_space=pltpu.VMEM)
    hbm = pl.BlockSpec(memory_space=pltpu.HBM)

    mine = hop(panel_blocks)
    theirs = cross(panel_blocks)
    own = pl.pallas_call(
        load_kernel,
        out_shape=jax.ShapeDtypeStruct(inverse_tiles.shape, inverse_tiles.dtype),
        in_specs=[hbm],
        out_specs=vmem,
        scratch_shapes=[pltpu.SemaphoreType.DMA],
        compiler_params=pltpu.CompilerParams(vmem_limit_bytes=4 << 20),
        name="load",
    )(inverse_tiles)
    other = cross(inverse_tiles)
    shards = [(0, panel_blocks), (1, mine)]
    for step in range(1, ways + 1):
        if step <= backs:
            theirs = hop(theirs)
        if step < ways:
            mine = hop(mine)
        if step <= backs:
            shards.append((-step, cross(theirs)))
        if step < ways:
            shards.append((step + 1, mine))
    late = [shard for shard in shards if shard[0] in (ways, -backs)]
    tail = len(late)

    tile = size * size
    small = pltpu.CompilerParams(vmem_limit_bytes=8 << 20)
    shape = jax.ShapeDtypeStruct
    sums = ()
    for step in range(2, ways + 1):
        batch = [x for x in shards if x[0] in ((0, 1) if step == 2 else (step - 1, 2 - step))]
        sums = pl.pallas_call(
            functools.partial(add_kernel, grid_rows, [k for k, _ in batch], not sums),
            out_shape=(
                shape((supers, rows * size, size), jnp.float32),
                shape((supers, rows * size, size), jnp.bfloat16),
            ),
            in_specs=[smem] * 2 + [vmem] * (2 + len(batch) + len(sums)),
            out_specs=(vmem, vmem),
            input_output_aliases={4 + len(batch) + i: i for i in range(len(sums))},
            compiler_params=small,
            cost_estimate=pl.CostEstimate(
                flops=2 * supers * len(batch) * per * rows * tile * size,
                bytes_accessed=2 * supers * len(batch) * per * (rows + 1) * tile,
                transcendentals=0,
            ),
            name="add",
        )(structure, block_slot, own, other, *[x for _, x in batch], *sums)
    tiles, marks = [], []
    for sup in range(supers):
        made = pl.pallas_call(
            functools.partial(prepare_kernel, grid_rows, sup, [k for k, _ in late]),
            out_shape=(
                shape((tail * per, rows * size, size), jnp.bfloat16),
                shape((rows + tail * per * rows, size), jnp.float32),
            ),
            in_specs=[smem] * 2 + [vmem] * 2,
            out_specs=(vmem,) * 2,
            compiler_params=small,
            cost_estimate=pl.CostEstimate(
                flops=0, bytes_accessed=4 * tail * per * rows * tile, transcendentals=0
            ),
            name="prepare",
        )(structure, block_slot, own, other)
        tiles.append(made[0])
        marks.append(made[1])
    first = jnp.full((1, size), lax.axis_index("prow") == 0, jnp.float32)

    sigma, value = pl.pallas_call(
        functools.partial(finish_kernel, supers, tail * per),
        out_shape=(
            shape((supers, rows, size, size), jnp.bfloat16),
            shape(diag_inverse.shape, jnp.float32),
        ),
        in_specs=[vmem] * (4 + 2 * supers + tail),
        out_specs=(vmem, vmem),
        compiler_params=small,
        cost_estimate=pl.CostEstimate(
            flops=2 * supers * tail * per * rows * tile * size,
            bytes_accessed=supers * rows * tile * 8,
            transcendentals=0,
        ),
        name="finish",
    )(diag_inverse, first, *sums, *tiles, *marks, *[x for _, x in late])

    sigma = pl.pallas_call(
        load_kernel,
        out_shape=shape(sigma.shape, sigma.dtype),
        in_specs=[vmem],
        out_specs=hbm,
        scratch_shapes=[pltpu.SemaphoreType.DMA],
        compiler_params=pltpu.CompilerParams(vmem_limit_bytes=4 << 20),
        name="store",
    )(sigma)

    stride = 1
    while stride < grid_rows:
        value = value + lax.ppermute(value, "prow", [(i, i ^ stride) for i in range(grid_rows)])
        stride *= 2
    return sigma, value


def solution(mesh):
    in_specs = (
        P(("fields", "prow"), "pcol", None, None),
        P("fields", "prow", None, "pcol"),
        P("fields", "pcol"),
        P("fields", None),
        P("fields"),
    )
    out_specs = (P("fields", "prow", None, "pcol"), P("fields", "pcol"))
    grid_rows = mesh.shape["prow"]

    def body(*args):
        return per_device(grid_rows, *args)

    return jax.shard_map(body, mesh=mesh, in_specs=in_specs, out_specs=out_specs, check_vma=False)
```

```python
import functools
import jax
import jax.numpy as jnp
from jax import lax
from jax.experimental import pallas as pl
from jax.experimental.pallas import tpu as pltpu
from jax.sharding import PartitionSpec as P

AXES = ("prow", "pcol")


def ring_order(size):
    return list(range(0, size, 2)) + [i for i in range(size - 1, 0, -1) if i % 2]


def ring_pairs(size):
    order = ring_order(size)
    pairs = []
    for place, row in enumerate(order):
        pairs.append((row * 2, order[(place + 1) % size] * 2))
        pairs.append((row * 2 + 1, order[(place - 1) % size] * 2 + 1))
    return pairs


class Place:
    def __init__(self, size):
        self.size = size
        self.prow = lax.axis_index("prow")
        self.pcol = lax.axis_index("pcol")
        odd = self.prow & 1
        half = self.prow >> 1
        self.at = half + odd * (size - 1 - 2 * half)

    def row(self, steps):
        if steps == 0:
            return self.prow
        at = lax.rem(self.at + self.size - steps * (1 - 2 * self.pcol), self.size)
        return jnp.where(2 * at < self.size, 2 * at, 2 * (self.size - 1 - at) + 1)


def load_kernel(source, target, sem):
    copy = pltpu.make_async_copy(source, target, sem)
    copy.start()
    copy.wait()


def prepare_kernel(grid_rows, s, late, structure, block_slot, own, other, late_tiles, marks):
    place = Place(grid_rows)
    rows, cols, size = own.shape[0], own.shape[1], own.shape[2]
    count = late_tiles.shape[0]
    per = count // len(late)
    slots = [block_slot[structure[s, place.row(k) * per + i]] for k in late for i in range(per)]
    every = [block_slot[structure[s, b]] for b in range(structure.shape[1])]
    for r in range(rows):
        row = place.prow * rows + r
        used = functools.reduce(jnp.logical_or, [slot == row for slot in every])
        marks[pl.ds(r, 1)] = jnp.full((1, size), -used.astype(jnp.float32))
        for i, slot in enumerate(slots):
            hit = (slot == row).astype(jnp.float32)
            marks[pl.ds(rows + i * rows + r, 1)] = jnp.full((1, size), hit)
    for i, slot in enumerate(slots):
        at = lax.rem(slot, cols)
        for r in range(rows):
            late_tiles[i, pl.ds(r * size, size)] = jnp.where(slot // cols == place.pcol, own[r, at], other[r, at])


def add_kernel(grid_rows, steps, fresh, structure, block_slot, own, other, *refs):
    panels, (acc, own_panel) = refs[:len(steps)], refs[-2:]
    place = Place(grid_rows)
    rows, cols, size = own.shape[0], own.shape[1], own.shape[2]
    supers, per = panels[0].shape[0], panels[0].shape[1]
    if fresh:
        own_panel[...] = jnp.zeros_like(own_panel)
    shard_rows = [place.row(k) * per for k in steps]
    blocks = [(panel, k) for panel in panels for k in range(per)]
    slots = [[block_slot[structure[s, at + k]] for at in shard_rows for k in range(per)] for s in range(supers)]
    for s in range(supers):
        for r in range(rows):
            for slot, (panel, k) in zip(slots[s], blocks):

                @pl.when(slot == place.prow * rows + r)
                def _():
                    own_panel[s, pl.ds(r * size, size)] = panel[s, k]

    for s in range(supers):
        for r in range(rows):
            here = pl.ds(r * size, size)
            total = None if fresh else acc[s, here]
            for slot, (panel, k) in zip(slots[s], blocks):
                at = lax.rem(slot, cols)
                tile = jnp.where(slot // cols == place.pcol, own[r, at], other[r, at])
                part = jnp.dot(tile, panel[s, k], preferred_element_type=jnp.float32)
                total = part if total is None else total + part
            acc[s, here] = total


def finish_kernel(supers, count, diag, first, acc, own_panel, *refs):
    tiles, marks, refs = refs[:supers], refs[supers:2 * supers], refs[2 * supers:]
    panels, (sigma, value) = refs[:-2], refs[-2:]
    rows, size = sigma.shape[1], sigma.shape[2]
    blocks = [(panel, k) for panel in panels for k in range(count // len(panels))]
    for s in range(supers):
        result = diag[pl.ds(s, 1)] * first[...]
        for r in range(rows):
            here = pl.ds(r * size, size)
            total = acc[s, here]
            for i, (panel, k) in enumerate(blocks):
                total = total + jnp.dot(tiles[s][i, here], panel[s, k], preferred_element_type=jnp.float32)
            total = total * marks[s][pl.ds(r, 1)]
            sigma[s, r] = total.astype(sigma.dtype)
            weight = own_panel[s, here].astype(jnp.float32)
            for i, (panel, k) in enumerate(blocks):
                weight = weight + marks[s][pl.ds(rows + i * rows + r, 1)] * panel[s, k].astype(jnp.float32)
            result = result - jnp.sum(weight * total, axis=0, keepdims=True)
        value[pl.ds(s, 1)] = result


def per_device(grid_rows, inverse_tiles, panel_blocks, diag_inverse, structure, block_slot):
    rows, size = inverse_tiles.shape[0], inverse_tiles.shape[2]
    supers, per = panel_blocks.shape[0], panel_blocks.shape[1]
    pairs = ring_pairs(grid_rows)
    swap = [(i, i ^ 1) for i in range(2 * grid_rows)]
    ways, backs = grid_rows // 2, (grid_rows - 1) // 2

    def hop(x):
        return lax.ppermute(x, AXES, pairs)

    def cross(x):
        return lax.ppermute(x, AXES, swap)

    smem = pl.BlockSpec(memory_space=pltpu.SMEM)
    vmem = pl.BlockSpec(memory_space=pltpu.VMEM)
    hbm = pl.BlockSpec(memory_space=pltpu.HBM)

    mine = hop(panel_blocks)
    theirs = cross(panel_blocks)
    own = pl.pallas_call(
        load_kernel,
        out_shape=jax.ShapeDtypeStruct(inverse_tiles.shape, inverse_tiles.dtype),
        in_specs=[hbm],
        out_specs=vmem,
        scratch_shapes=[pltpu.SemaphoreType.DMA],
        compiler_params=pltpu.CompilerParams(vmem_limit_bytes=4 << 20),
        name="load",
    )(inverse_tiles)
    other = cross(inverse_tiles)
    shards = [(0, panel_blocks), (1, mine)]
    for step in range(1, ways + 1):
        if step <= backs:
            theirs = hop(theirs)
        if step < ways:
            mine = hop(mine)
        if step <= backs:
            shards.append((-step, cross(theirs)))
        if step < ways:
            shards.append((step + 1, mine))
    late = [shard for shard in shards if shard[0] in (ways, -backs)]
    tail = len(late)

    tile = size * size
    small = pltpu.CompilerParams(vmem_limit_bytes=8 << 20)
    shape = jax.ShapeDtypeStruct
    sums = ()
    for step in range(2, ways + 1):
        batch = [x for x in shards if x[0] in ((0, 1) if step == 2 else (step - 1, 2 - step))]
        sums = pl.pallas_call(
            functools.partial(add_kernel, grid_rows, [k for k, _ in batch], not sums),
            out_shape=(
                shape((supers, rows * size, size), jnp.float32),
                shape((supers, rows * size, size), jnp.bfloat16),
            ),
            in_specs=[smem] * 2 + [vmem] * (2 + len(batch) + len(sums)),
            out_specs=(vmem, vmem),
            input_output_aliases={4 + len(batch) + i: i for i in range(len(sums))},
            compiler_params=small,
            cost_estimate=pl.CostEstimate(
                flops=2 * supers * len(batch) * per * rows * tile * size,
                bytes_accessed=2 * supers * len(batch) * per * (rows + 1) * tile,
                transcendentals=0,
            ),
            name="add",
        )(structure, block_slot, own, other, *[x for _, x in batch], *sums)
    tiles, marks = [], []
    for sup in range(supers):
        made = pl.pallas_call(
            functools.partial(prepare_kernel, grid_rows, sup, [k for k, _ in late]),
            out_shape=(
                shape((tail * per, rows * size, size), jnp.bfloat16),
                shape((rows + tail * per * rows, size), jnp.float32),
            ),
            in_specs=[smem] * 2 + [vmem] * 2,
            out_specs=(vmem,) * 2,
            compiler_params=small,
            cost_estimate=pl.CostEstimate(
                flops=0, bytes_accessed=4 * tail * per * rows * tile, transcendentals=0
            ),
            name="prepare",
        )(structure, block_slot, own, other)
        tiles.append(made[0])
        marks.append(made[1])
    first = jnp.full((1, size), lax.axis_index("prow") == 0, jnp.float32)

    sigma, value = pl.pallas_call(
        functools.partial(finish_kernel, supers, tail * per),
        out_shape=(
            shape((supers, rows, size, size), jnp.bfloat16),
            shape(diag_inverse.shape, jnp.float32),
        ),
        in_specs=[vmem] * (4 + 2 * supers + tail),
        out_specs=(vmem, vmem),
        compiler_params=small,
        cost_estimate=pl.CostEstimate(
            flops=2 * supers * tail * per * rows * tile * size,
            bytes_accessed=supers * rows * tile * 8,
            transcendentals=0,
        ),
        name="finish",
    )(diag_inverse, first, *sums, *tiles, *marks, *[x for _, x in late])

    sigma = pl.pallas_call(
        load_kernel,
        out_shape=shape(sigma.shape, sigma.dtype),
        in_specs=[vmem],
        out_specs=hbm,
        scratch_shapes=[pltpu.SemaphoreType.DMA],
        compiler_params=pltpu.CompilerParams(vmem_limit_bytes=4 << 20),
        name="store",
    )(sigma)

    def swapped(x, stride):
        return lax.ppermute(x, "prow", [(i, i ^ stride) for i in range(grid_rows)])

    if grid_rows % 4 == 0:
        value = (value + swapped(value, 1)) + (swapped(value, 2) + swapped(value, 3))
        stride = 4
    else:
        stride = 1
    while stride < grid_rows:
        value = value + swapped(value, stride)
        stride *= 2
    return sigma, value


def solution(mesh):
    in_specs = (
        P(("fields", "prow"), "pcol", None, None),
        P("fields", "prow", None, "pcol"),
        P("fields", "pcol"),
        P("fields", None),
        P("fields"),
    )
    out_specs = (P("fields", "prow", None, "pcol"), P("fields", "pcol"))
    grid_rows = mesh.shape["prow"]

    def body(*args):
        return per_device(grid_rows, *args)

    return jax.shard_map(body, mesh=mesh, in_specs=in_specs, out_specs=out_specs, check_vma=False)
```
